128 devices in a mesh: row: 16 (over y_hi, z, core), col: 8 (over x, y_lo).
Axes of the slice: x: 4, y: 4 (y_hi: 2, y_lo: 2; y = y_hi * 2 + y_lo), z: 4, core: 2. Of those that a mesh axis runs over, the one named last changes fastest.
Arguments:
- pivot_inverse: float32 [1024, 1024], P('row'), may hold values from -1 to 2, as said below
- panel: float32 [32, 1024, 1024], P('row', 'col'), may hold values from -1 to 1
- trailing: float32 [320, 1024, 1024], P('row', None, 'col'), may hold values from -6 to 6
- tile_list: int32 [320, 2], P('row'), may hold values from -1 to 31, as said below
Outputs:
- solved_panel: float32 [32, 1024, 1024], P('row', 'col')
- updated: float32 [320, 1024, 1024], P('row', None, 'col')
The draws below stay inside these ranges and needn't reach their ends.
Inputs may be any that keep to these rules, and one draw needn't show every extreme that they name: `pivot_inverse`: lower triangular, diagonal between 0.5 and 2. `tile_list`: slots t of group g are g * 20 to g * 20 + 19. Column 0 lies in 0 to 1; column 1 is a panel tile or -1 for an empty slot. The live slots of a group come first and name distinct pairs; each group in the first half of the groups holds exactly 6 live slots, each in the second half exactly 20. Empty slots hold 0 in column 0.
All inputs are finite; a program needn't handle non-finite values.
Results may differ from the reference program's by a relative error of at most 0.00007.
Values sent between devices are 32-bit elements; how exact they have to be, the bound alone decides.
No kernel may reach another device: no remote copies, remote signals or barrier semaphores. Data moves between devices by JAX's collectives and lax.ppermute only.
A program may use at most 128 MiB of HBM per device.

```python
import math
import jax
import jax.numpy as jnp
from jax import lax

B = 1024
PAN_DEV = 2
TR_DEV = 20
LIGHT = 6
PANEL = 32
TRAIL = 320


def draw_pivot_inverse(key, part):
    first_key, second_key = jax.random.split(key)
    lower_part = jnp.tril(jax.random.normal(first_key, (B, B), jnp.float32), -1) * (0.6 / math.sqrt(B))
    diagonal = jnp.exp(jax.random.uniform(second_key, (B,), jnp.float32, math.log(0.5), math.log(2.0)))
    return (lower_part + jnp.diag(diagonal)).astype(jnp.float32)


def draw_tile_list(key, part):
    groups = TRAIL // TR_DEV
    options = PAN_DEV * PANEL
    group_keys = jax.random.split(jax.random.fold_in(key, 7), groups)
    shuffled = jax.vmap(lambda one_key: jax.random.permutation(one_key, options))(group_keys)[:, :TR_DEV]
    local_tile = shuffled // PANEL
    paired_tile = shuffled % PANEL
    slot_index = jnp.arange(TR_DEV)[None, :]
    group_index = jnp.arange(groups)[:, None]
    live_count = jnp.where(group_index >= groups // 2, TR_DEV, LIGHT)
    live_slot = slot_index < live_count
    local_tile = jnp.where(live_slot, local_tile, 0)
    paired_tile = jnp.where(live_slot, paired_tile, -1)
    return jnp.stack([local_tile, paired_tile], -1).reshape(TRAIL, 2).astype(jnp.int32)


def steps_of(rng, extent, pieces, least, high):
    level, own = 1.0, jax.random.fold_in(rng, 6)
    for axis_at, shards_of in pieces:
        steps = jnp.exp(jax.random.uniform(jax.random.fold_in(own, axis_at), (shards_of,), jnp.float32, least / len(pieces), high / len(pieces)))
        level = level * jnp.repeat(steps, extent[axis_at] // shards_of).reshape([-1 if axis == axis_at else 1 for axis in range(len(extent))])
    return level


def noise(own_key, shape, deviation, reach, cuts=(), kind=jnp.bfloat16):
    loudness = steps_of(own_key, shape, cuts, -0.22, 0.18) if cuts else 1.0
    values = jax.random.normal(own_key, shape, jnp.float32) * deviation * loudness
    return jnp.minimum(jnp.maximum(values, -reach), reach).astype(kind)


def setup_inputs(seed: int = 0) -> dict:
    seeds = jax.random.split(jax.random.key(seed), 5)
    pivot_inverse = draw_pivot_inverse(jax.random.fold_in(seeds[4], 71), 0)
    panel = noise(seeds[1], (PANEL, B, B), 0.18, 1.0, ((0, 16), (1, 8)), jnp.float32)
    trailing = noise(seeds[2], (TRAIL, B, B), 1.0, 6.0, ((0, 16), (2, 8)), jnp.float32)
    tile_list = draw_tile_list(jax.random.fold_in(seeds[4], 71), 0)
    return {"pivot_inverse": pivot_inverse, "panel": panel, "trailing": trailing, "tile_list": tile_list}


highest = lax.Precision.HIGHEST


def reference(pivot_inverse, panel, trailing, tile_list):
    solved = jnp.einsum("pak,jk->paj", panel, pivot_inverse, precision=highest)
    group_index = jnp.arange(TRAIL, dtype=jnp.int32) // TR_DEV
    row_tile = (group_index * PAN_DEV + tile_list[:, 0]).astype(jnp.int32)
    col_tile = jnp.maximum(tile_list[:, 1], 0).astype(jnp.int32)
    live_slot = tile_list[:, 1] >= 0

    def update_slot(packed):
        current, left_index, right_index, live_flag = packed
        product = jnp.einsum("ak,bk->ab", solved[left_index], solved[right_index], precision=highest)
        return current - jnp.where(live_flag, product, jnp.zeros_like(product))

    updated = lax.map(update_slot, (trailing, row_tile, col_tile, live_slot))
    return solved, updated
```

```python
import functools

import jax
import jax.numpy as jnp
from jax import lax
from jax.experimental import pallas as pl
from jax.experimental.pallas import tpu as pltpu
from jax.sharding import PartitionSpec as P

SLOTS = 20
ROWS = 128
ORDER = 1024
AXES = ("row", "col")
high = lax.Precision.HIGH


def place(index):
    row, col = divmod(index, 8)
    return col // 2, (row // 8) * 2 + col % 2, (row // 2) % 4, row % 2


def index_of(x, y, z, core):
    return (((y // 2) * 4 + z) * 2 + core) * 8 + x * 2 + y % 2


def send(value, move):
    pairs = [(i, index_of(*move(*place(i)))) for i in range(128)]
    return lax.ppermute(value, AXES, pairs)


def to_sibling(x, y, z, core):
    return x, y, z, 1 - core


def along_z(x, y, z, core):
    return x, y, (z + 1 - 2 * core) % 4, core


def along_x(x, y, z, core):
    return (x + 1 - 2 * core) % 4, y, z, core


def far_y(x, y, z, core):
    return x, (y + 2) % 4, z, core


def near_y(x, y, z, core):
    return x, y ^ 1, z, core


def gather_pivot(rows):
    swap = functools.partial(send, move=to_sibling)
    far = send(rows, far_y)
    pair = jnp.concatenate([rows, far], 0)
    chip = jnp.concatenate([pair, swap(pair)], 0)
    z1 = send(chip, along_z)
    z2 = send(z1[:128], along_z)
    sz1 = swap(z1)
    sz2 = swap(z2)
    return chip, z1, sz1, z2, sz2


def pivot_whole(parts, far, z, core):
    chip, z1, sz1, z2, sz2 = parts
    order = jnp.concatenate([chip, z1, sz1, z2, sz2], 0).reshape(16, 64, ORDER)
    block = jnp.arange(16, dtype=jnp.int32)
    block_far, block_z, block_core = block // 8, (block // 2) % 4, block % 2
    near = (block_far != far).astype(jnp.int32)
    dz = (block_z - z) % 4
    other = (block_core != core).astype(jnp.int32)
    mine = jnp.where(core == 0, dz == 3, dz == 1)
    at = jnp.where(
        dz == 0,
        near + 2 * other,
        jnp.where(
            dz == 2,
            12 + near + 2 * other,
            jnp.where(mine, 4 + near + 2 * other, 8 + near + 2 * (1 - other)),
        ),
    )
    return order[at].reshape(ORDER, ORDER)


def update_kernel(order, left, buffer, position, live, rows_at, *refs):
    trailing, hi_own, lo_own, hi_far, lo_far = refs[:5]
    sources = refs[5:17]
    out = refs[17]
    slab, sems = refs[18:]
    step = pl.program_id(0)

    def fetch(at):
        half = at % 2
        for which, source in enumerate(sources):
            @pl.when(buffer[at] == which)
            def _():
                pltpu.make_async_copy(source.at[position[at]], slab.at[half], sems.at[half]).start()

    @pl.when(jnp.logical_and(step == 0, live[0] == 1))
    def _():
        fetch(0)

    after = jnp.minimum(step + 1, SLOTS - 1)

    @pl.when(jnp.logical_and(step + 1 < SLOTS, live[after] == 1))
    def _():
        fetch(after)

    @pl.when(live[step] == 1)
    def _():
        half = step % 2
        pltpu.make_async_copy(sources[0].at[0], slab.at[half], sems.at[half]).wait()
        right = slab[half]
        right_hi = right.astype(jnp.bfloat16)
        right_lo = (right - right_hi.astype(jnp.float32)).astype(jnp.bfloat16)
        both = jnp.concatenate([right_hi, right_lo], 0)
        dims = (((1,), (1,)), ((), ()))
        for base, (hi, lo) in enumerate(((hi_own, lo_own), (hi_far, lo_far))):
            term = lax.dot_general(hi[0], both, dims, preferred_element_type=jnp.float32)
            term += lax.dot_general(lo[0], both, dims, preferred_element_type=jnp.float32)
            total = term[:, :ROWS] + term[:, ROWS:]
            for j in range(4):
                at = pl.ds(pl.multiple_of(rows_at[base * 4 + j], ROWS), ROWS)
                out[0, at, :] = trailing[0, at, :] - total[j * ROWS : (j + 1) * ROWS]

    @pl.when(live[step] == 0)
    def _():
        out[...] = trailing[...]


def update(trailing, lefts, sources, tables):
    def slot(step, order, *_):
        return order[step], 0, 0

    def tile(step, order, left, *_):
        return left[step], 0, 0

    slot_spec = pl.BlockSpec((1, ORDER, ROWS), slot)
    left_spec = pl.BlockSpec((1, ORDER // 2, ORDER), tile)
    return pl.pallas_call(
        update_kernel,
        grid_spec=pltpu.PrefetchScalarGridSpec(
            num_scalar_prefetch=6,
            grid=(SLOTS,),
            in_specs=[slot_spec] + [left_spec] * 4 + [pl.BlockSpec(memory_space=pl.ANY)] * 12,
            out_specs=slot_spec,
            scratch_shapes=[pltpu.VMEM((2, ROWS, ORDER), jnp.float32), pltpu.SemaphoreType.DMA((2,))],
        ),
        out_shape=jax.ShapeDtypeStruct(trailing.shape, trailing.dtype),
        compiler_params=pltpu.CompilerParams(vmem_limit_bytes=48 << 20),
    )(*tables, trailing, *lefts, *sources)


def halves(blocks, square):
    stacked = jnp.stack(blocks, 1)
    product = jnp.einsum("pxak,kj->pxaj", stacked, square, precision=high)
    top = lax.reduce_precision(product, 8, 7)
    flat = (2, 4 * ROWS, ORDER)
    return top.astype(jnp.bfloat16).reshape(flat), (product - top).astype(jnp.bfloat16).reshape(flat)


def per_device(pivot_inverse, panel, trailing, tile_list):
    row, col = lax.axis_index("row"), lax.axis_index("col")
    far, z, core = row // 8, (row // 2) % 4, row % 2
    x, near = col // 2, col % 2
    swap = functools.partial(send, move=to_sibling)

    sib = swap(panel)
    chip = jnp.concatenate([panel, sib], 0)
    near_own = send(panel, near_y)
    x1 = send(chip, along_x)
    pivot_parts = gather_pivot(pivot_inverse)
    z1 = send(chip, along_z)
    near_chip = jnp.concatenate([near_own, swap(near_own)], 0)
    far_own = send(panel, far_y)
    x2 = send(x1[:2], along_x)
    sx1 = swap(x1[2:])
    nx1 = send(near_chip, along_x)
    z2 = send(z1[:2], along_z)
    sz1 = swap(z1)
    far_sib = swap(far_own)
    far_chip = jnp.concatenate([far_own, far_sib], 0)
    fz1 = send(far_chip, along_z)
    nx2 = send(nx1[:2], along_x)
    nsx1 = swap(nx1[2:])
    sz2 = swap(z2)
    fz2 = send(z2, far_y)
    sfz1 = swap(fz1)
    sfz2 = swap(fz2)

    full_pivot = pivot_whole(pivot_parts, far, z, core)
    solved = jnp.einsum("pak,jk->paj", panel, full_pivot, precision=high)
    square = jnp.einsum("ki,kj->ij", full_pivot, full_pivot, precision=high)
    lefts = halves([panel, x1[:2], sx1, x2], square) + halves([near_own, nx1[:2], nsx1, nx2], square)
    toward = jnp.where(core == 0, -1, 1)
    shifts = jnp.stack([x, (x + toward) % 4, (x - toward) % 4, (x + 2) % 4])
    rows_at = jnp.concatenate([(shifts * 2 + near) * ROWS, (shifts * 2 + 1 - near) * ROWS]).astype(jnp.int32)

    left, right = tile_list[:, 0], tile_list[:, 1]
    live = right >= 0
    key = jnp.where(live, left, 2) * SLOTS + jnp.arange(SLOTS, dtype=jnp.int32)
    rank = jnp.sum((key[None, :] < key[:, None]).astype(jnp.int32), 1)
    pick = (rank[None, :] == jnp.arange(SLOTS, dtype=jnp.int32)[:, None]).astype(jnp.int32)
    order = jnp.sum(pick * jnp.arange(SLOTS, dtype=jnp.int32)[None, :], 1)
    left = jnp.sum(pick * jnp.where(live, left, 1)[None, :], 1)
    right = jnp.sum(pick * jnp.maximum(right, 0)[None, :], 1)
    live = jnp.sum(pick * live.astype(jnp.int32)[None, :], 1)
    inner, owner = right % 2, right // 2
    owner_far, owner_z, owner_core = owner // 8, (owner // 2) % 4, owner % 2
    dz = (owner_z - z) % 4
    other = (owner_core != core).astype(jnp.int32)
    mine = jnp.where(core == 0, dz == 3, dz == 1)
    buffer = jnp.where(dz == 0, other, jnp.where(dz == 2, 2 + other, jnp.where(mine, 4, 5)))
    buffer = buffer + jnp.where(owner_far != far, 6, 0)
    position = inner + jnp.where(dz % 2 == 0, 0, 2 * jnp.where(mine, other, 1 - other))

    sources = [panel, sib, z2, sz2, z1, sz1, far_own, far_sib, fz2, sfz2, fz1, sfz1]
    tables = [t.astype(jnp.int32) for t in (order, left, buffer, position, live)] + [rows_at]
    return solved, update(trailing, lefts, sources, tables)


def solution(mesh):
    placed = (P("row", None), P("row", "col", None), P("row", None, "col"), P("row", None))
    return jax.shard_map(
        per_device,
        mesh=mesh,
        in_specs=placed,
        out_specs=(P("row", "col", None), P("row", None, "col")),
        check_vma=False,
    )
```

```python
import functools

import jax
import jax.numpy as jnp
from jax import lax
from jax.experimental import pallas as pl
from jax.experimental.pallas import tpu as pltpu
from jax.sharding import PartitionSpec as P

SLOTS = 20
STEPS = 12
ROWS = 128
ORDER = 1024
AXES = ("row", "col")
high = lax.Precision.HIGH


def place(index):
    row, col = divmod(index, 8)
    return col // 2, (row // 8) * 2 + col % 2, (row // 2) % 4, row % 2


def index_of(x, y, z, core):
    return (((y // 2) * 4 + z) * 2 + core) * 8 + x * 2 + y % 2


def send(value, move):
    pairs = [(i, index_of(*move(*place(i)))) for i in range(128)]
    return lax.ppermute(value, AXES, pairs)


def to_sibling(x, y, z, core):
    return x, y, z, 1 - core


def along_z(x, y, z, core):
    return x, y, (z + 1 - 2 * core) % 4, core


def along_x(x, y, z, core):
    return (x + 1 - 2 * core) % 4, y, z, core


def far_y(x, y, z, core):
    return x, (y + 2) % 4, z, core


def near_y(x, y, z, core):
    return x, y ^ 1, z, core


def after(value, *first):
    return lax.optimization_barrier((value,) + first)[0]


def turn_z(by):
    return lambda x, y, z, core: (x, y, (z + by) % 4, core)


def solve(panel, lower, upper, z):
    half = ORDER // 2
    first = jnp.einsum("pak,jk->paj", panel[:, :, :half], upper, precision=high)
    second = jnp.einsum("pak,jk->paj", panel, lower, precision=high)

    def turned(cols):
        twice = jnp.concatenate([cols, cols], 2)
        return lax.dynamic_slice_in_dim(twice, (half - z * ROWS) % half, half, 2)

    return jnp.concatenate([turned(first), turned(second)], 2)


def square_of(lower, upper):
    half = ORDER // 2
    whole = jnp.einsum("ki,kj->ij", lower, lower, precision=high)
    corner = jnp.einsum("ki,kj->ij", upper, upper, precision=high)
    return whole.at[:half, :half].add(corner)


def update_kernel(counts, slots, left, buffer, position, kind, meta, *refs):
    blocks, n_sources = counts
    trails, refs = refs[:2], refs[2:]
    lefts, refs = refs[: 2 * len(blocks)], refs[2 * len(blocks) :]
    sources, refs = refs[:n_sources], refs[n_sources:]
    out, slab, sems, done, done_sems = refs
    step = pl.program_id(0)
    half = step % 2

    def fetch(at):
        for which, source in enumerate(sources):
            for q in range(2):
                @pl.when(buffer[2 * at + q] == which)
                def _():
                    pltpu.make_async_copy(
                        source.at[position[2 * at + q]], slab.at[at % 2, q], sems.at[at % 2, q]
                    ).start()

    def written(at, q):
        return pltpu.make_async_copy(
            done.at[at % 2, q], out.at[slots[2 * at + q]], done_sems.at[at % 2, q]
        )

    @pl.when(jnp.logical_and(step == 0, kind[0] == 2))
    def _():
        fetch(0)

    following = jnp.minimum(step + 1, STEPS - 1)

    @pl.when(jnp.logical_and(step + 1 < STEPS, kind[2 * following] == 2))
    def _():
        fetch(following)

    before = jnp.maximum(step - 2, 0)
    for q in range(2):
        @pl.when(jnp.logical_and(step >= 2, kind[2 * before + q] > 0))
        def _():
            written(before, q).wait()

    @pl.when(kind[2 * step] == 2)
    def _():
        tops, rests = [], []
        for q in range(2):
            pltpu.make_async_copy(sources[0].at[0], slab.at[half, q], sems.at[half, q]).wait()
            right = slab[half, q]
            top = right.astype(jnp.bfloat16)
            tops.append(top)
            rests.append((right - top.astype(jnp.float32)).astype(jnp.bfloat16))
        top, rest = jnp.concatenate(tops, 0), jnp.concatenate(rests, 0)
        first = 0
        for at, size in enumerate(blocks):
            hi, lo = lefts[2 * at][0], lefts[2 * at + 1][0]
            term = product(hi, top) + product(hi, rest) + product(lo, top)
            for j in range(size):
                lane = pl.ds(pl.multiple_of(meta[first + j], ROWS), ROWS)
                rows = slice(j * ROWS, (j + 1) * ROWS)
                for q in range(2):
                    done[half, q, lane, :] = trails[q][0, lane, :] - term[rows, q * ROWS : (q + 1) * ROWS]
            first += size

    @pl.when(kind[2 * step] == 1)
    def _():
        for q in range(2):
            done[half, q] = trails[q][0]

    for q in range(2):
        @pl.when(kind[2 * step + q] > 0)
        def _():
            written(step, q).start()

    @pl.when(step == STEPS - 1)
    def _():
        for at in (STEPS - 2, STEPS - 1):
            for q in range(2):
                @pl.when(kind[2 * at + q] > 0)
                def _():
                    written(at, q).wait()


def product(a, b):
    return lax.dot_general(a, b, (((1,), (1,)), ((), ())), preferred_element_type=jnp.float32)


def update(trailing, blocks, lefts, sources, tables):
    def slot(q):
        return lambda step, slots, *_: (slots[2 * step + q], 0, 0)

    def tile(step, slots, left, *_):
        return left[step], 0, 0

    left_specs = [pl.BlockSpec((1, p.shape[1], ORDER), tile) for p in lefts]
    hbm = pl.BlockSpec(memory_space=pl.ANY)
    return pl.pallas_call(
        functools.partial(update_kernel, (blocks, len(sources))),
        grid_spec=pltpu.PrefetchScalarGridSpec(
            num_scalar_prefetch=len(tables),
            grid=(STEPS,),
            in_specs=[pl.BlockSpec((1, ORDER, ROWS), slot(q)) for q in range(2)]
            + left_specs
            + [hbm] * len(sources),
            out_specs=hbm,
            scratch_shapes=[
                pltpu.VMEM((2, 2, ROWS, ORDER), jnp.float32),
                pltpu.SemaphoreType.DMA((2, 2)),
                pltpu.VMEM((2, 2, ORDER, ROWS), jnp.float32),
                pltpu.SemaphoreType.DMA((2, 2)),
            ],
        ),
        out_shape=jax.ShapeDtypeStruct(trailing.shape, trailing.dtype),
        compiler_params=pltpu.CompilerParams(vmem_limit_bytes=56 << 20),
    )(*tables, trailing, trailing, *lefts, *sources)


def split(product):
    top = lax.reduce_precision(product, 8, 7)
    flat = (2, product.shape[1] * ROWS, ORDER)
    return top.astype(jnp.bfloat16).reshape(flat), (product - top).astype(jnp.bfloat16).reshape(flat)


def times(blocks, square):
    return split(jnp.einsum("pxak,kj->pxaj", jnp.stack(blocks, 1), square, precision=high))


def per_device(pivot_inverse, panel, trailing, tile_list):
    row, col = lax.axis_index("row"), lax.axis_index("col")
    far, z, core = row // 8, (row // 2) % 4, row % 2
    x, near = col // 2, col % 2
    swap = functools.partial(send, move=to_sibling)

    toward = jnp.where(core == 0, -1, 1)
    places = jnp.stack([x, (x + toward) % 4, (x - toward) % 4, (x + 2) % 4]) * 2
    places = jnp.concatenate([places + near, places + 1 - near]) * ROWS
    left, right = tile_list[:, 0], tile_list[:, 1]
    live = right >= 0
    right = jnp.maximum(right, 0)
    inner, owner = right % 2, right // 2
    owner_far, owner_z, owner_core = owner // 8, (owner // 2) % 4, owner % 2
    dz = (owner_z - z) % 4
    other_core = (owner_core != core).astype(jnp.int32)
    ahead = jnp.where(core == 0, dz == 3, dz == 1)
    here = jnp.where(dz % 2 == 0, dz + other_core, jnp.where(ahead, 4 + other_core, 7 - other_core))
    there = jnp.where(dz % 2 == 0, 8 + dz + other_core, jnp.where(dz == 3, 12, 13) + 2 * other_core)
    buffer = jnp.where(owner_far == far, here, there)
    group = jnp.where(live, left, 2)
    slot = jnp.arange(SLOTS, dtype=jnp.int32)
    ahead_of = (group[None, :] == group[:, None]) & (slot[None, :] < slot[:, None])
    rank = jnp.sum(ahead_of.astype(jnp.int32), 1)
    pairs = [(jnp.sum((group == g).astype(jnp.int32)) + 1) // 2 for g in range(3)]
    start = jnp.where(group == 0, 0, jnp.where(group == 1, pairs[0], pairs[0] + pairs[1]))
    at = 2 * start + rank
    spots = jnp.arange(2 * STEPS, dtype=jnp.int32)
    pick = (at[None, :] == spots[:, None]).astype(jnp.int32)
    mate = (at[None, :] == (spots ^ 1)[:, None]).astype(jnp.int32)
    rows = jnp.stack([slot, buffer, inner, jnp.where(live, 2, 1)]).astype(jnp.int32)
    mine_rows = jnp.sum(rows[:, None, :] * pick[None], 2)
    mate_rows = jnp.sum(rows[:, None, :] * mate[None], 2)
    filled = jnp.sum(pick, 1)
    chosen = jnp.where(filled[None] > 0, mine_rows, mate_rows)
    kind = jnp.where(filled > 0, chosen[3], 0)
    left_of = jnp.where(jnp.arange(STEPS, dtype=jnp.int32) < pairs[0], 0, 1).astype(jnp.int32)
    tables = [chosen[0], left_of, chosen[1], chosen[2], kind, places.astype(jnp.int32)]

    half = ORDER // 2

    sib = swap(panel)
    other = send(pivot_inverse, far_y)
    near_own = send(after(panel, other), near_y)
    z1a = send(panel, along_z)
    upper = jnp.where(far == 0, pivot_inverse, other)[:, :half]
    lower = jnp.where(far == 0, other, pivot_inverse)
    mine = jnp.concatenate([lower, upper], 1)
    chip = jnp.concatenate([panel, sib], 0)
    x1 = send(chip, along_x)
    z1b = send(after(sib, z1a), along_z)
    from_down = send(mine, turn_z(1))
    from_up = send(mine, turn_z(-1))

    done = (x1, z1a, z1b, near_own, from_down, from_up, *tables)
    z2 = send(after(z1a, *done), along_z)
    across = send(after(mine, *done), turn_z(2))
    x2n = send(after(jnp.concatenate([x1[:2], near_own], 0), *done), along_x)
    far_own = send(after(panel, *done), far_y)
    near_sib = swap(near_own)
    sx1, sz1a, sz1b = swap(x1[2:]), swap(z1a), swap(z1b)
    x2, nx1a = x2n[:2], x2n[2:]

    done = (z2, across, x2n, far_own, near_sib, sx1, sz1a, sz1b)
    quarters = after(jnp.stack([mine, from_up, across, from_down], 0), *done)
    theirs = swap(quarters)
    nx12 = send(after(jnp.concatenate([near_sib, nx1a], 0), *done), along_x)
    fz_down = send(after(far_own, *done), turn_z(1))
    fz_up = send(after(far_own, *done), turn_z(-1))
    fz2 = send(after(z2, *done), far_y)
    sz2, far_sib = swap(after(z2, theirs)), swap(after(far_own, theirs))
    nx1b, nx2 = nx12[:2], nx12[2:]

    first = jnp.where(core == 0, quarters, theirs)
    second = jnp.where(core == 0, theirs, quarters)
    whole = jnp.stack([first, second], 1).reshape(half, ORDER + half)
    lower, upper = whole[:, :ORDER], whole[:, ORDER:]
    square = square_of(lower, upper)
    own_left = times([panel, x1[:2], sx1, x2], square)
    near_first = times([near_own, nx1a], square)
    solved = solve(panel, lower, upper, z)
    nsx1 = swap(after(nx1b, solved, *own_left, *near_first))
    near_second = times([nsx1, nx2], square)
    sfz_down, sfz_up, sfz2 = swap(after(fz_down, solved, *own_left, *near_first)), swap(fz_up), swap(fz2)

    sources = [panel, sib, z2, sz2, z1a, z1b, sz1a, sz1b]
    sources += [far_own, far_sib, fz2, sfz2, fz_down, fz_up, sfz_down, sfz_up]
    lefts = own_left + near_first + near_second
    return solved, update(trailing, (4, 2, 2), lefts, sources, tables)


def solution(mesh):
    placed = (P("row", None), P("row", "col", None), P("row", None, "col"), P("row", None))
    return jax.shard_map(
        per_device,
        mesh=mesh,
        in_specs=placed,
        out_specs=(P("row", "col", None), P("row", None, "col")),
        check_vma=False,
    )
```

```python
import functools

import jax
import jax.numpy as jnp
from jax import lax
from jax.experimental import pallas as pl
from jax.experimental.pallas import tpu as pltpu
from jax.sharding import PartitionSpec as P

SLOTS = 20
STEPS = 12
ROWS = 128
ORDER = 1024
AXES = ("row", "col")
high = lax.Precision.HIGH


def place(index):
    row, col = divmod(index, 8)
    return col // 2, (row // 8) * 2 + col % 2, (row // 2) % 4, row % 2


def index_of(x, y, z, core):
    return (((y // 2) * 4 + z) * 2 + core) * 8 + x * 2 + y % 2


def send(value, move):
    pairs = [(i, index_of(*move(*place(i)))) for i in range(128)]
    return lax.ppermute(value, AXES, pairs)


def to_sibling(x, y, z, core):
    return x, y, z, 1 - core


def along_z(x, y, z, core):
    return x, y, (z + 1 - 2 * core) % 4, core


def along_x(x, y, z, core):
    return (x + 1 - 2 * core) % 4, y, z, core


def far_y(x, y, z, core):
    return x, (y + 2) % 4, z, core


def near_y(x, y, z, core):
    return x, y ^ 1, z, core


def after(value, *first):
    return lax.optimization_barrier((value,) + first)[0]


def turn_z(by):
    return lambda x, y, z, core: (x, y, (z + by) % 4, core)


def solve(panel, lower, upper, z):
    half = ORDER // 2
    first = jnp.einsum("pak,jk->paj", panel[:, :, :half], upper, precision=high)
    second = jnp.einsum("pak,jk->paj", panel, lower, precision=high)

    def turned(cols):
        twice = jnp.concatenate([cols, cols], 2)
        return lax.dynamic_slice_in_dim(twice, (half - z * ROWS) % half, half, 2)

    return jnp.concatenate([turned(first), turned(second)], 2)


def square_of(lower, upper):
    half = ORDER // 2
    whole = jnp.einsum("ki,kj->ij", lower, lower, precision=high)
    corner = jnp.einsum("ki,kj->ij", upper, upper, precision=high)
    return whole.at[:half, :half].add(corner)


def update_kernel(counts, slots, left, buffer, position, kind, meta, *refs):
    blocks, n_sources = counts
    trails, refs = refs[:2], refs[2:]
    lefts, refs = refs[: 2 * len(blocks)], refs[2 * len(blocks) :]
    sources, refs = refs[:n_sources], refs[n_sources:]
    out, slab, sems, done, done_sems = refs
    step = pl.program_id(0)
    half = step % 2

    def fetch(at):
        for which, source in enumerate(sources):
            for q in range(2):
                @pl.when(buffer[2 * at + q] == which)
                def _():
                    pltpu.make_async_copy(
                        source.at[position[2 * at + q]], slab.at[at % 2, q], sems.at[at % 2, q]
                    ).start()

    def written(at, q):
        return pltpu.make_async_copy(
            done.at[at % 2, q], out.at[slots[2 * at + q]], done_sems.at[at % 2, q]
        )

    @pl.when(jnp.logical_and(step == 0, kind[0] == 2))
    def _():
        fetch(0)

    following = jnp.minimum(step + 1, STEPS - 1)

    @pl.when(jnp.logical_and(step + 1 < STEPS, kind[2 * following] == 2))
    def _():
        fetch(following)

    before = jnp.maximum(step - 2, 0)
    for q in range(2):
        @pl.when(jnp.logical_and(step >= 2, kind[2 * before + q] > 0))
        def _():
            written(before, q).wait()

    @pl.when(kind[2 * step] == 2)
    def _():
        tops, rests = [], []
        for q in range(2):
            pltpu.make_async_copy(sources[0].at[0], slab.at[half, q], sems.at[half, q]).wait()
            right = slab[half, q]
            top = right.astype(jnp.bfloat16)
            tops.append(top)
            rests.append((right - top.astype(jnp.float32)).astype(jnp.bfloat16))
        top, rest = jnp.concatenate(tops, 0), jnp.concatenate(rests, 0)
        first = 0
        for at, size in enumerate(blocks):
            hi, lo = lefts[2 * at][0], lefts[2 * at + 1][0]
            term = product(hi, top) + product(hi, rest) + product(lo, top)
            for j in range(size):
                lane = pl.ds(pl.multiple_of(meta[first + j], ROWS), ROWS)
                rows = slice(j * ROWS, (j + 1) * ROWS)
                for q in range(2):
                    done[half, q, lane, :] = trails[q][0, lane, :] - term[rows, q * ROWS : (q + 1) * ROWS]
            first += size

    @pl.when(kind[2 * step] == 1)
    def _():
        for q in range(2):
            done[half, q] = trails[q][0]

    for q in range(2):
        @pl.when(kind[2 * step + q] > 0)
        def _():
            written(step, q).start()

    @pl.when(step == STEPS - 1)
    def _():
        for at in (STEPS - 2, STEPS - 1):
            for q in range(2):
                @pl.when(kind[2 * at + q] > 0)
                def _():
                    written(at, q).wait()


def product(a, b):
    return lax.dot_general(a, b, (((1,), (1,)), ((), ())), preferred_element_type=jnp.float32)


def update(trailing, blocks, lefts, sources, tables):
    def slot(q):
        return lambda step, slots, *_: (slots[2 * step + q], 0, 0)

    def tile(step, slots, left, *_):
        return left[step], 0, 0

    left_specs = [pl.BlockSpec((1, p.shape[1], ORDER), tile) for p in lefts]
    hbm = pl.BlockSpec(memory_space=pl.ANY)
    return pl.pallas_call(
        functools.partial(update_kernel, (blocks, len(sources))),
        grid_spec=pltpu.PrefetchScalarGridSpec(
            num_scalar_prefetch=len(tables),
            grid=(STEPS,),
            in_specs=[pl.BlockSpec((1, ORDER, ROWS), slot(q)) for q in range(2)]
            + left_specs
            + [hbm] * len(sources),
            out_specs=hbm,
            scratch_shapes=[
                pltpu.VMEM((2, 2, ROWS, ORDER), jnp.float32),
                pltpu.SemaphoreType.DMA((2, 2)),
                pltpu.VMEM((2, 2, ORDER, ROWS), jnp.float32),
                pltpu.SemaphoreType.DMA((2, 2)),
            ],
        ),
        out_shape=jax.ShapeDtypeStruct(trailing.shape, trailing.dtype),
        compiler_params=pltpu.CompilerParams(vmem_limit_bytes=56 << 20),
    )(*tables, trailing, trailing, *lefts, *sources)


def split(product):
    top = lax.reduce_precision(product, 8, 7)
    flat = (2, product.shape[1] * ROWS, ORDER)
    return top.astype(jnp.bfloat16).reshape(flat), (product - top).astype(jnp.bfloat16).reshape(flat)


def times(blocks, square):
    return split(jnp.einsum("pxak,kj->pxaj", jnp.stack(blocks, 1), square, precision=high))


def per_device(pivot_inverse, panel, trailing, tile_list):
    row, col = lax.axis_index("row"), lax.axis_index("col")
    far, z, core = row // 8, (row // 2) % 4, row % 2
    x, near = col // 2, col % 2
    swap = functools.partial(send, move=to_sibling)

    toward = jnp.where(core == 0, -1, 1)
    places = jnp.stack([x, (x + toward) % 4, (x - toward) % 4, (x + 2) % 4]) * 2
    places = jnp.concatenate([places + near, places + 1 - near]) * ROWS
    left, right = tile_list[:, 0], tile_list[:, 1]
    live = right >= 0
    right = jnp.maximum(right, 0)
    inner, owner = right % 2, right // 2
    owner_far, owner_z, owner_core = owner // 8, (owner // 2) % 4, owner % 2
    dz = (owner_z - z) % 4
    other_core = (owner_core != core).astype(jnp.int32)
    ahead = jnp.where(core == 0, dz == 3, dz == 1)
    here = jnp.where(dz % 2 == 0, dz + other_core, jnp.where(ahead, 4 + other_core, 7 - other_core))
    there = jnp.where(dz % 2 == 0, 8 + dz + other_core, jnp.where(dz == 3, 12, 13) + 2 * other_core)
    buffer = jnp.where(owner_far == far, here, there)
    group = jnp.where(live, left, 2)
    slot = jnp.arange(SLOTS, dtype=jnp.int32)
    ahead_of = (group[None, :] == group[:, None]) & (slot[None, :] < slot[:, None])
    rank = jnp.sum(ahead_of.astype(jnp.int32), 1)
    pairs = [(jnp.sum((group == g).astype(jnp.int32)) + 1) // 2 for g in range(3)]
    start = jnp.where(group == 0, 0, jnp.where(group == 1, pairs[0], pairs[0] + pairs[1]))
    at = 2 * start + rank
    spots = jnp.arange(2 * STEPS, dtype=jnp.int32)
    pick = (at[None, :] == spots[:, None]).astype(jnp.int32)
    mate = (at[None, :] == (spots ^ 1)[:, None]).astype(jnp.int32)
    rows = jnp.stack([slot, buffer, inner, jnp.where(live, 2, 1)]).astype(jnp.int32)
    mine_rows = jnp.sum(rows[:, None, :] * pick[None], 2)
    mate_rows = jnp.sum(rows[:, None, :] * mate[None], 2)
    filled = jnp.sum(pick, 1)
    chosen = jnp.where(filled[None] > 0, mine_rows, mate_rows)
    kind = jnp.where(filled > 0, chosen[3], 0)
    left_of = jnp.where(jnp.arange(STEPS, dtype=jnp.int32) < pairs[0], 0, 1).astype(jnp.int32)
    tables = [chosen[0], left_of, chosen[1], chosen[2], kind, places.astype(jnp.int32)]

    half = ORDER // 2

    sib = swap(panel)
    other = send(pivot_inverse, far_y)
    near_own = send(after(panel, other), near_y)
    z1a = send(panel, along_z)
    upper = jnp.where(far == 0, pivot_inverse, other)[:, :half]
    lower = jnp.where(far == 0, other, pivot_inverse)
    mine = jnp.concatenate([lower, upper], 1)
    chip = jnp.concatenate([panel, sib], 0)
    x1 = send(chip, along_x)
    z1b = send(after(sib, z1a), along_z)
    from_down = send(mine, turn_z(1))
    from_up = send(mine, turn_z(-1))

    done = (x1, z1a, z1b, near_own, from_down, from_up, *tables)
    z2 = send(after(z1a, *done), along_z)
    across = send(after(mine, *done), turn_z(2))
    x2n = send(after(jnp.concatenate([x1[:2], near_own], 0), *done), along_x)
    far_own = send(after(panel, *done), far_y)
    quarters = jnp.stack([mine, from_up, across, from_down], 0)
    both_sib = swap(after(jnp.concatenate([near_own, x1[2:]], 0), *done))
    near_sib, sx1 = both_sib[:2], both_sib[2:]
    x2, nx1a = x2n[:2], x2n[2:]

    done = (z2, across, x2n, far_own, both_sib)
    near_pair = after(jnp.concatenate([near_sib, nx1a], 0), *done)
    nx12 = send(near_pair, along_x)
    theirs = swap(after(quarters, near_pair))
    sz1a, sz1b = swap(after(z1a, theirs)), swap(after(z1b, theirs))
    fz_down = send(after(far_own, near_pair), turn_z(1))
    fz_up = send(after(far_own, near_pair), turn_z(-1))
    fz2 = send(after(z2, near_pair), far_y)
    sz2, far_sib = swap(after(z2, theirs)), swap(after(far_own, theirs))
    nx1b, nx2 = nx12[:2], nx12[2:]

    first = jnp.where(core == 0, quarters, theirs)
    second = jnp.where(core == 0, theirs, quarters)
    whole = jnp.stack([first, second], 1).reshape(half, ORDER + half)
    lower, upper = whole[:, :ORDER], whole[:, ORDER:]
    square = square_of(lower, upper)
    own_left = times([panel, x1[:2], sx1, x2], square)
    near_first = times([near_own, nx1a], square)
    solved = solve(panel, lower, upper, z)
    ready = (solved, *own_left, *near_first)
    nsx1 = swap(after(nx1b, *ready))
    near_second = times([nsx1, nx2], square)
    sfz_down, sfz_up, sfz2 = [swap(after(part, *ready)) for part in (fz_down, fz_up, fz2)]

    sources = [panel, sib, z2, sz2, z1a, z1b, sz1a, sz1b]
    sources += [far_own, far_sib, fz2, sfz2, fz_down, fz_up, sfz_down, sfz_up]
    lefts = own_left + near_first + near_second
    return solved, update(trailing, (4, 2, 2), lefts, sources, tables)


def solution(mesh):
    placed = (P("row", None), P("row", "col", None), P("row", None, "col"), P("row", None))
    return jax.shard_map(
        per_device,
        mesh=mesh,
        in_specs=placed,
        out_specs=(P("row", "col", None), P("row", None, "col")),
        check_vma=False,
    )
```

```python
import functools

import jax
import jax.numpy as jnp
from jax import lax
from jax.experimental import pallas as pl
from jax.experimental.pallas import tpu as pltpu
from jax.sharding import PartitionSpec as P

SLOTS = 20
STEPS = 12
ROWS = 128
ORDER = 1024
AXES = ("row", "col")
high = lax.Precision.HIGH


def place(index):
    row, col = divmod(index, 8)
    return col // 2, (row // 8) * 2 + col % 2, (row // 2) % 4, row % 2


def index_of(x, y, z, core):
    return (((y // 2) * 4 + z) * 2 + core) * 8 + x * 2 + y % 2


def send(value, move):
    pairs = [(i, index_of(*move(*place(i)))) for i in range(128)]
    return lax.ppermute(value, AXES, pairs)


def to_sibling(x, y, z, core):
    return x, y, z, 1 - core


def along_z(x, y, z, core):
    return x, y, (z + 1 - 2 * core) % 4, core


def along_x(x, y, z, core):
    return (x + 1 - 2 * core) % 4, y, z, core


def far_y(x, y, z, core):
    return x, (y + 2) % 4, z, core


def near_y(x, y, z, core):
    return x, y ^ 1, z, core


def after(value, *first):
    return lax.optimization_barrier((value,) + first)[0]


def turn_z(by):
    return lambda x, y, z, core: (x, y, (z + by) % 4, core)


def solve(panel, lower, upper, z):
    half = ORDER // 2
    first = jnp.einsum("pak,jk->paj", panel[:, :, :half], upper, precision=high)
    second = jnp.einsum("pak,jk->paj", panel, lower, precision=high)

    def turned(cols):
        twice = jnp.concatenate([cols, cols], 2)
        return lax.dynamic_slice_in_dim(twice, (half - z * ROWS) % half, half, 2)

    return jnp.concatenate([turned(first), turned(second)], 2)


def square_of(lower, upper):
    half = ORDER // 2
    whole = jnp.einsum("ki,kj->ij", lower, lower, precision=high)
    corner = jnp.einsum("ki,kj->ij", upper, upper, precision=high)
    return whole.at[:half, :half].add(corner)


def update_kernel(counts, slots, left, buffer, position, kind, meta, *refs):
    blocks, n_sources = counts
    trails, refs = refs[:2], refs[2:]
    lefts, refs = refs[: 2 * len(blocks)], refs[2 * len(blocks) :]
    sources, refs = refs[:n_sources], refs[n_sources:]
    out, slab, sems, done, done_sems = refs
    step = pl.program_id(0)
    half = step % 2

    def fetch(at):
        for which, source in enumerate(sources):
            for q in range(2):
                @pl.when(buffer[2 * at + q] == which)
                def _():
                    pltpu.make_async_copy(
                        source.at[position[2 * at + q]], slab.at[at % 2, q], sems.at[at % 2, q]
                    ).start()

    def written(at, q):
        return pltpu.make_async_copy(
            done.at[at % 2, q], out.at[slots[2 * at + q]], done_sems.at[at % 2, q]
        )

    @pl.when(jnp.logical_and(step == 0, kind[0] == 2))
    def _():
        fetch(0)

    following = jnp.minimum(step + 1, STEPS - 1)

    @pl.when(jnp.logical_and(step + 1 < STEPS, kind[2 * following] == 2))
    def _():
        fetch(following)

    before = jnp.maximum(step - 2, 0)
    for q in range(2):
        @pl.when(jnp.logical_and(step >= 2, kind[2 * before + q] > 0))
        def _():
            written(before, q).wait()

    @pl.when(kind[2 * step] == 2)
    def _():
        tops, rests = [], []
        for q in range(2):
            pltpu.make_async_copy(sources[0].at[0], slab.at[half, q], sems.at[half, q]).wait()
            right = slab[half, q]
            top = right.astype(jnp.bfloat16)
            tops.append(top)
            rests.append((right - top.astype(jnp.float32)).astype(jnp.bfloat16))
        top, rest = jnp.concatenate(tops, 0), jnp.concatenate(rests, 0)
        first = 0
        for at, size in enumerate(blocks):
            hi, lo = lefts[2 * at][0], lefts[2 * at + 1][0]
            term = product(hi, top) + product(hi, rest) + product(lo, top)
            for j in range(size):
                lane = pl.ds(pl.multiple_of(meta[first + j], ROWS), ROWS)
                rows = slice(j * ROWS, (j + 1) * ROWS)
                for q in range(2):
                    done[half, q, lane, :] = trails[q][0, lane, :] - term[rows, q * ROWS : (q + 1) * ROWS]
            first += size

    @pl.when(kind[2 * step] == 1)
    def _():
        for q in range(2):
            done[half, q] = trails[q][0]

    for q in range(2):
        @pl.when(kind[2 * step + q] > 0)
        def _():
            written(step, q).start()

    @pl.when(step == STEPS - 1)
    def _():
        for at in (STEPS - 2, STEPS - 1):
            for q in range(2):
                @pl.when(kind[2 * at + q] > 0)
                def _():
                    written(at, q).wait()


def product(a, b):
    return lax.dot_general(a, b, (((1,), (1,)), ((), ())), preferred_element_type=jnp.float32)


def update(trailing, blocks, lefts, sources, tables):
    def slot(q):
        return lambda step, slots, *_: (slots[2 * step + q], 0, 0)

    def tile(step, slots, left, *_):
        return left[step], 0, 0

    left_specs = [pl.BlockSpec((1, p.shape[1], ORDER), tile) for p in lefts]
    hbm = pl.BlockSpec(memory_space=pl.ANY)
    return pl.pallas_call(
        functools.partial(update_kernel, (blocks, len(sources))),
        grid_spec=pltpu.PrefetchScalarGridSpec(
            num_scalar_prefetch=len(tables),
            grid=(STEPS,),
            in_specs=[pl.BlockSpec((1, ORDER, ROWS), slot(q)) for q in range(2)]
            + left_specs
            + [hbm] * len(sources),
            out_specs=hbm,
            scratch_shapes=[
                pltpu.VMEM((2, 2, ROWS, ORDER), jnp.float32),
                pltpu.SemaphoreType.DMA((2, 2)),
                pltpu.VMEM((2, 2, ORDER, ROWS), jnp.float32),
                pltpu.SemaphoreType.DMA((2, 2)),
            ],
        ),
        out_shape=jax.ShapeDtypeStruct(trailing.shape, trailing.dtype),
        compiler_params=pltpu.CompilerParams(vmem_limit_bytes=56 << 20),
    )(*tables, trailing, trailing, *lefts, *sources)


def split(product):
    top = lax.reduce_precision(product, 8, 7)
    flat = (2, product.shape[1] * ROWS, ORDER)
    return top.astype(jnp.bfloat16).reshape(flat), (product - top).astype(jnp.bfloat16).reshape(flat)


def times(blocks, square):
    return split(jnp.einsum("pxak,kj->pxaj", jnp.stack(blocks, 1), square, precision=high))


def per_device(pivot_inverse, panel, trailing, tile_list):
    row, col = lax.axis_index("row"), lax.axis_index("col")
    far, z, core = row // 8, (row // 2) % 4, row % 2
    x, near = col // 2, col % 2
    swap = functools.partial(send, move=to_sibling)

    toward = jnp.where(core == 0, -1, 1)
    places = jnp.stack([x, (x + toward) % 4, (x - toward) % 4, (x + 2) % 4]) * 2
    places = jnp.concatenate([places + near, places + 1 - near]) * ROWS
    left, right = tile_list[:, 0], tile_list[:, 1]
    live = right >= 0
    right = jnp.maximum(right, 0)
    inner, owner = right % 2, right // 2
    owner_far, owner_z, owner_core = owner // 8, (owner // 2) % 4, owner % 2
    dz = (owner_z - z) % 4
    other_core = (owner_core != core).astype(jnp.int32)
    ahead = jnp.where(core == 0, dz == 3, dz == 1)
    here = jnp.where(dz % 2 == 0, dz + other_core, jnp.where(ahead, 4 + other_core, 7 - other_core))
    there = jnp.where(dz % 2 == 0, 8 + dz + other_core, jnp.where(dz == 3, 12, 13) + 2 * other_core)
    buffer = jnp.where(owner_far == far, here, there)
    group = jnp.where(live, left, 2)
    slot = jnp.arange(SLOTS, dtype=jnp.int32)
    ahead_of = (group[None, :] == group[:, None]) & (slot[None, :] < slot[:, None])
    rank = jnp.sum(ahead_of.astype(jnp.int32), 1)
    pairs = [(jnp.sum((group == g).astype(jnp.int32)) + 1) // 2 for g in range(3)]
    start = jnp.where(group == 0, 0, jnp.where(group == 1, pairs[0], pairs[0] + pairs[1]))
    at = 2 * start + rank
    spots = jnp.arange(2 * STEPS, dtype=jnp.int32)
    pick = (at[None, :] == spots[:, None]).astype(jnp.int32)
    mate = (at[None, :] == (spots ^ 1)[:, None]).astype(jnp.int32)
    rows = jnp.stack([slot, buffer, inner, jnp.where(live, 2, 1)]).astype(jnp.int32)
    mine_rows = jnp.sum(rows[:, None, :] * pick[None], 2)
    mate_rows = jnp.sum(rows[:, None, :] * mate[None], 2)
    filled = jnp.sum(pick, 1)
    chosen = jnp.where(filled[None] > 0, mine_rows, mate_rows)
    kind = jnp.where(filled > 0, chosen[3], 0)
    left_of = jnp.where(jnp.arange(STEPS, dtype=jnp.int32) < pairs[0], 0, 1).astype(jnp.int32)
    tables = [chosen[0], left_of, chosen[1], chosen[2], kind, places.astype(jnp.int32)]

    half = ORDER // 2

    sib = swap(panel)
    other = send(pivot_inverse, far_y)
    near_own = send(after(panel, other), near_y)
    z1a = send(panel, along_z)
    upper = jnp.where(far == 0, pivot_inverse, other)[:, :half]
    lower = jnp.where(far == 0, other, pivot_inverse)
    mine = jnp.concatenate([lower, upper], 1)
    x1a = send(panel, along_x)
    x1b = send(after(sib, x1a), along_x)
    z1b = send(after(sib, z1a), along_z)
    from_down = send(mine, turn_z(1))
    from_up = send(mine, turn_z(-1))

    done = (x1a, x1b, z1a, z1b, near_own, from_down, from_up, *tables)
    z2 = send(after(z1a, *done), along_z)
    across = send(after(mine, *done), turn_z(2))
    x2n = send(after(jnp.concatenate([x1a, near_own], 0), *done), along_x)
    far_own = send(after(panel, *done), far_y)
    quarters = jnp.stack([mine, from_up, across, from_down], 0)
    both_sib = swap(after(jnp.concatenate([near_own, x1b], 0), *done))
    near_sib, sx1 = both_sib[:2], both_sib[2:]
    x2, nx1a = x2n[:2], x2n[2:]

    done = (z2, across, x2n, far_own, both_sib)
    near_pair = after(jnp.concatenate([near_sib, nx1a], 0), *done)
    nx12 = send(near_pair, along_x)
    theirs = swap(after(quarters, near_pair))
    sz1a, sz1b = swap(after(z1a, theirs)), swap(after(z1b, theirs))
    fz_down = send(after(far_own, near_pair), turn_z(1))
    fz_up = send(after(far_own, near_pair), turn_z(-1))
    fz2 = send(after(z2, near_pair), far_y)
    sz2, far_sib = swap(after(z2, theirs)), swap(after(far_own, theirs))
    nx1b, nx2 = nx12[:2], nx12[2:]

    first = jnp.where(core == 0, quarters, theirs)
    second = jnp.where(core == 0, theirs, quarters)
    whole = jnp.stack([first, second], 1).reshape(half, ORDER + half)
    lower, upper = whole[:, :ORDER], whole[:, ORDER:]
    square = square_of(lower, upper)
    own_first = times([panel, x1a], square)
    own_second = times([sx1, x2], square)
    near_first = times([near_own, nx1a], square)
    solved = solve(panel, lower, upper, z)
    ready = (solved, *own_first, *near_first)
    nsx1 = swap(after(nx1b, *ready))
    near_second = times([nsx1, nx2], square)
    sfz_down, sfz_up, sfz2 = [swap(after(part, *ready, *own_second)) for part in (fz_down, fz_up, fz2)]

    sources = [panel, sib, z2, sz2, z1a, z1b, sz1a, sz1b]
    sources += [far_own, far_sib, fz2, sfz2, fz_down, fz_up, sfz_down, sfz_up]
    lefts = own_first + own_second + near_first + near_second
    return solved, update(trailing, (2, 2, 2, 2), lefts, sources, tables)


def solution(mesh):
    placed = (P("row", None), P("row", "col", None), P("row", None, "col"), P("row", None))
    return jax.shard_map(
        per_device,
        mesh=mesh,
        in_specs=placed,
        out_specs=(P("row", "col", None), P("row", None, "col")),
        check_vma=False,
    )
```

```python
import functools

import jax
import jax.numpy as jnp
from jax import lax
from jax.experimental import pallas as pl
from jax.experimental.pallas import tpu as pltpu
from jax.sharding import PartitionSpec as P

SLOTS = 20
STEPS = 12
ROWS = 128
ORDER = 1024
AXES = ("row", "col")
high = lax.Precision.HIGH


def place(index):
    row, col = divmod(index, 8)
    return col // 2, (row // 8) * 2 + col % 2, (row // 2) % 4, row % 2


def index_of(x, y, z, core):
    return (((y // 2) * 4 + z) * 2 + core) * 8 + x * 2 + y % 2


def send(value, move):
    pairs = [(i, index_of(*move(*place(i)))) for i in range(128)]
    return lax.ppermute(value, AXES, pairs)


def to_sibling(x, y, z, core):
    return x, y, z, 1 - core


def along_z(x, y, z, core):
    return x, y, (z + 1 - 2 * core) % 4, core


def along_x(x, y, z, core):
    return (x + 1 - 2 * core) % 4, y, z, core


def far_y(x, y, z, core):
    return x, (y + 2) % 4, z, core


def near_y(x, y, z, core):
    return x, y ^ 1, z, core


def after(value, *first):
    return lax.optimization_barrier((value,) + first)[0]


def turn_z(by):
    return lambda x, y, z, core: (x, y, (z + by) % 4, core)


def solve(panel, lower, upper, z):
    half = ORDER // 2
    first = jnp.einsum("pak,jk->paj", panel[:, :, :half], upper, precision=high)
    second = jnp.einsum("pak,jk->paj", panel, lower, precision=high)

    def turned(cols):
        twice = jnp.concatenate([cols, cols], 2)
        return lax.dynamic_slice_in_dim(twice, (half - z * ROWS) % half, half, 2)

    return jnp.concatenate([turned(first), turned(second)], 2)


def square_of(lower, upper):
    half = ORDER // 2
    whole = jnp.einsum("ki,kj->ij", lower, lower, precision=high)
    corner = jnp.einsum("ki,kj->ij", upper, upper, precision=high)
    return whole.at[:half, :half].add(corner)


def update_kernel(counts, slots, left, buffer, position, kind, meta, *refs):
    n_lefts, n_sources = counts
    trails, refs = refs[:2], refs[2:]
    lefts, refs = refs[:n_lefts], refs[n_lefts:]
    sources, refs = refs[:n_sources], refs[n_sources:]
    out, slab, sems, done, done_sems, whole_left, left_sems = refs
    step = pl.program_id(0)
    half = step % 2

    def fetch(at):
        for which, source in enumerate(sources):
            for q in range(2):
                @pl.when(buffer[2 * at + q] == which)
                def _():
                    pltpu.make_async_copy(
                        source.at[position[2 * at + q]], slab.at[at % 2, q], sems.at[at % 2, q]
                    ).start()

    def left_copies(tile):
        depth = ORDER // (n_lefts // 2)
        for at, source in enumerate(lefts):
            rows = pl.ds(at // 2 * depth, depth)
            yield pltpu.make_async_copy(
                source.at[tile], whole_left.at[tile, at % 2, rows, :], left_sems.at[tile, at]
            )

    @pl.when(step == 0)
    def _():
        for tile in range(2):
            for copy in left_copies(tile):
                copy.start()

    def written(at, q):
        return pltpu.make_async_copy(
            done.at[at % 2, q], out.at[slots[2 * at + q]], done_sems.at[at % 2, q]
        )

    @pl.when(jnp.logical_and(step == 0, kind[0] == 2))
    def _():
        fetch(0)

    following = jnp.minimum(step + 1, STEPS - 1)

    @pl.when(jnp.logical_and(step + 1 < STEPS, kind[2 * following] == 2))
    def _():
        fetch(following)

    before = jnp.maximum(step - 2, 0)
    for q in range(2):
        @pl.when(jnp.logical_and(step >= 2, kind[2 * before + q] > 0))
        def _():
            written(before, q).wait()

    for tile in range(2):
        @pl.when(step == meta[8 + tile])
        def _():
            for copy in left_copies(tile):
                copy.wait()

    @pl.when(kind[2 * step] == 2)
    def _():
        tops, rests = [], []
        for q in range(2):
            pltpu.make_async_copy(sources[0].at[0], slab.at[half, q], sems.at[half, q]).wait()
            right = slab[half, q]
            top = right.astype(jnp.bfloat16)
            tops.append(top)
            rests.append((right - top.astype(jnp.float32)).astype(jnp.bfloat16))
        top, rest = jnp.concatenate(tops, 0), jnp.concatenate(rests, 0)
        hi, lo = whole_left[left[step], 0], whole_left[left[step], 1]
        term = product(hi, top) + product(hi, rest) + product(lo, top)
        for j in range(ORDER // ROWS):
            lane = pl.ds(pl.multiple_of(meta[j], ROWS), ROWS)
            rows = slice(j * ROWS, (j + 1) * ROWS)
            for q in range(2):
                done[half, q, lane, :] = trails[q][0, lane, :] - term[rows, q * ROWS : (q + 1) * ROWS]

    @pl.when(kind[2 * step] == 1)
    def _():
        for q in range(2):
            done[half, q] = trails[q][0]

    for q in range(2):
        @pl.when(kind[2 * step + q] > 0)
        def _():
            written(step, q).start()

    @pl.when(step == STEPS - 1)
    def _():
        for at in (STEPS - 2, STEPS - 1):
            for q in range(2):
                @pl.when(kind[2 * at + q] > 0)
                def _():
                    written(at, q).wait()


def product(a, b):
    return lax.dot_general(a, b, (((1,), (1,)), ((), ())), preferred_element_type=jnp.float32)


def update(trailing, lefts, sources, tables):
    def slot(q):
        return lambda step, slots, *_: (slots[2 * step + q], 0, 0)

    hbm = pl.BlockSpec(memory_space=pl.ANY)
    return pl.pallas_call(
        functools.partial(update_kernel, (len(lefts), len(sources))),
        grid_spec=pltpu.PrefetchScalarGridSpec(
            num_scalar_prefetch=len(tables),
            grid=(STEPS,),
            in_specs=[pl.BlockSpec((1, ORDER, ROWS), slot(q)) for q in range(2)]
            + [hbm] * (len(lefts) + len(sources)),
            out_specs=hbm,
            scratch_shapes=[
                pltpu.VMEM((2, 2, ROWS, ORDER), jnp.float32),
                pltpu.SemaphoreType.DMA((2, 2)),
                pltpu.VMEM((2, 2, ORDER, ROWS), jnp.float32),
                pltpu.SemaphoreType.DMA((2, 2)),
                pltpu.VMEM((2, 2, ORDER, ORDER), jnp.bfloat16),
                pltpu.SemaphoreType.DMA((2, len(lefts))),
            ],
        ),
        out_shape=jax.ShapeDtypeStruct(trailing.shape, trailing.dtype),
        compiler_params=pltpu.CompilerParams(vmem_limit_bytes=56 << 20),
    )(*tables, trailing, trailing, *lefts, *sources)


def split(product):
    top = lax.reduce_precision(product, 8, 7)
    flat = (2, product.shape[1] * ROWS, ORDER)
    return top.astype(jnp.bfloat16).reshape(flat), (product - top).astype(jnp.bfloat16).reshape(flat)


def times(blocks, square):
    return split(jnp.einsum("pxak,kj->pxaj", jnp.stack(blocks, 1), square, precision=high))


def per_device(pivot_inverse, panel, trailing, tile_list):
    row, col = lax.axis_index("row"), lax.axis_index("col")
    far, z, core = row // 8, (row // 2) % 4, row % 2
    x, near = col // 2, col % 2
    swap = functools.partial(send, move=to_sibling)

    toward = jnp.where(core == 0, -1, 1)
    places = jnp.stack([x, (x + toward) % 4, (x - toward) % 4, (x + 2) % 4]) * 2
    places = jnp.concatenate([places + near, places + 1 - near]) * ROWS
    left, right = tile_list[:, 0], tile_list[:, 1]
    live = right >= 0
    right = jnp.maximum(right, 0)
    inner, owner = right % 2, right // 2
    owner_far, owner_z, owner_core = owner // 8, (owner // 2) % 4, owner % 2
    dz = (owner_z - z) % 4
    other_core = (owner_core != core).astype(jnp.int32)
    ahead = jnp.where(core == 0, dz == 3, dz == 1)
    here = jnp.where(dz % 2 == 0, dz + other_core, jnp.where(ahead, 4 + other_core, 7 - other_core))
    there = jnp.where(dz % 2 == 0, 8 + dz + other_core, jnp.where(dz == 3, 12, 13) + 2 * other_core)
    buffer = jnp.where(owner_far == far, here, there)
    group = jnp.where(live, left, 2)
    slot = jnp.arange(SLOTS, dtype=jnp.int32)
    ahead_of = (group[None, :] == group[:, None]) & (slot[None, :] < slot[:, None])
    rank = jnp.sum(ahead_of.astype(jnp.int32), 1)
    pairs = [(jnp.sum((group == g).astype(jnp.int32)) + 1) // 2 for g in range(3)]
    start = jnp.where(group == 0, 0, jnp.where(group == 1, pairs[0], pairs[0] + pairs[1]))
    at = 2 * start + rank
    spots = jnp.arange(2 * STEPS, dtype=jnp.int32)
    pick = (at[None, :] == spots[:, None]).astype(jnp.int32)
    mate = (at[None, :] == (spots ^ 1)[:, None]).astype(jnp.int32)
    rows = jnp.stack([slot, buffer, inner, jnp.where(live, 2, 1)]).astype(jnp.int32)
    mine_rows = jnp.sum(rows[:, None, :] * pick[None], 2)
    mate_rows = jnp.sum(rows[:, None, :] * mate[None], 2)
    filled = jnp.sum(pick, 1)
    chosen = jnp.where(filled[None] > 0, mine_rows, mate_rows)
    kind = jnp.where(filled > 0, chosen[3], 0)
    left_of = jnp.where(jnp.arange(STEPS, dtype=jnp.int32) < pairs[0], 0, 1).astype(jnp.int32)
    meta = jnp.concatenate([places, jnp.stack([jnp.zeros_like(pairs[0]), pairs[0]])]).astype(jnp.int32)
    tables = [chosen[0], left_of, chosen[1], chosen[2], kind, meta]

    half = ORDER // 2

    sib = swap(panel)
    other = send(pivot_inverse, far_y)
    near_own = send(after(panel, other), near_y)
    z1a = send(panel, along_z)
    upper = jnp.where(far == 0, pivot_inverse, other)[:, :half]
    lower = jnp.where(far == 0, other, pivot_inverse)
    mine = jnp.concatenate([lower, upper], 1)
    x1a = send(panel, along_x)
    x1b = send(sib, along_x)
    z1b = send(sib, along_z)
    mine = after(mine, x1a, z1a)
    from_down = send(mine, turn_z(1))
    from_up = send(mine, turn_z(-1))

    done = (x1a, x1b, z1a, z1b, near_own, from_down, from_up, *tables)
    z2 = send(after(z1a, *done), along_z)
    across = send(after(mine, *done), turn_z(2))
    x2n = send(after(jnp.concatenate([x1a, near_own], 0), *done), along_x)
    far_own = send(after(panel, *done), far_y)
    quarters = jnp.stack([mine, from_up, across, from_down], 0)
    both_sib = swap(after(jnp.concatenate([near_own, x1b], 0), *done))
    near_sib, sx1 = both_sib[:2], both_sib[2:]
    x2, nx1a = x2n[:2], x2n[2:]

    done = (z2, across, x2n, far_own, both_sib)
    near_pair = after(jnp.concatenate([near_sib, nx1a], 0), *done)
    nx12 = send(near_pair, along_x)
    theirs = swap(after(quarters, near_pair))
    sz1a, sz1b = swap(after(z1a, theirs)), swap(after(z1b, theirs))
    fz_down = send(after(far_own, near_pair), turn_z(1))
    fz_up = send(after(far_own, near_pair), turn_z(-1))
    fz2 = send(after(z2, near_pair), far_y)
    sz2, far_sib = swap(after(z2, theirs)), swap(after(far_own, theirs))
    nx1b, nx2 = nx12[:2], nx12[2:]

    first = jnp.where(core == 0, quarters, theirs)
    second = jnp.where(core == 0, theirs, quarters)
    whole = jnp.stack([first, second], 1).reshape(half, ORDER + half)
    lower, upper = whole[:, :ORDER], whole[:, ORDER:]
    square = square_of(lower, upper)
    own_first = times([panel, x1a], square)
    own_second = times([sx1, x2], square)
    near_first = times([near_own, nx1a], square)
    solved = solve(panel, lower, upper, z)
    ready = (solved, *own_first, *near_first)
    nsx1 = swap(after(nx1b, *ready))
    near_second = times([nsx1, nx2], square)
    sfz_down, sfz_up, sfz2 = [swap(after(part, *ready, *own_second)) for part in (fz_down, fz_up, fz2)]

    sources = [panel, sib, z2, sz2, z1a, z1b, sz1a, sz1b]
    sources += [far_own, far_sib, fz2, sfz2, fz_down, fz_up, sfz_down, sfz_up]
    lefts = own_first + own_second + near_first + near_second
    return solved, update(trailing, lefts, sources, tables)


def solution(mesh):
    placed = (P("row", None), P("row", "col", None), P("row", None, "col"), P("row", None))
    return jax.shard_map(
        per_device,
        mesh=mesh,
        in_specs=placed,
        out_specs=(P("row", "col", None), P("row", None, "col")),
        check_vma=False,
    )
```

```python
import functools

import jax
import jax.numpy as jnp
from jax import lax
from jax.experimental import pallas as pl
from jax.experimental.pallas import tpu as pltpu
from jax.sharding import PartitionSpec as P

SLOTS = 20
STEPS = 12
ROWS = 128
ORDER = 1024
AXES = ("row", "col")
high = lax.Precision.HIGH


def place(index):
    row, col = divmod(index, 8)
    return col // 2, (row // 8) * 2 + col % 2, (row // 2) % 4, row % 2


def index_of(x, y, z, core):
    return (((y // 2) * 4 + z) * 2 + core) * 8 + x * 2 + y % 2


def send(value, move):
    pairs = [(i, index_of(*move(*place(i)))) for i in range(128)]
    return lax.ppermute(value, AXES, pairs)


def to_sibling(x, y, z, core):
    return x, y, z, 1 - core


def along_z(x, y, z, core):
    return x, y, (z + 1 - 2 * core) % 4, core


def along_x(x, y, z, core):
    return (x + 1 - 2 * core) % 4, y, z, core


def far_y(x, y, z, core):
    return x, (y + 2) % 4, z, core


def near_y(x, y, z, core):
    return x, y ^ 1, z, core


def after(value, *first):
    return lax.optimization_barrier((value,) + first)[0]


def turn_z(by):
    return lambda x, y, z, core: (x, y, (z + by) % 4, core)


def solve(panel, lower, upper, z):
    half = ORDER // 2
    first = jnp.einsum("pak,jk->paj", panel[:, :, :half], upper, precision=high)
    second = jnp.einsum("pak,jk->paj", panel, lower, precision=high)

    def turned(cols):
        twice = jnp.concatenate([cols, cols], 2)
        return lax.dynamic_slice_in_dim(twice, (half - z * ROWS) % half, half, 2)

    return jnp.concatenate([turned(first), turned(second)], 2)


def square_of(lower, upper):
    half = ORDER // 2
    whole = jnp.einsum("ki,kj->ij", lower, lower, precision=high)
    corner = jnp.einsum("ki,kj->ij", upper, upper, precision=high)
    return whole.at[:half, :half].add(corner)


def update_kernel(counts, slots, left, buffer, position, kind, meta, *refs):
    n_lefts, n_sources = counts
    trails, refs = refs[:2], refs[2:]
    lefts, refs = refs[:n_lefts], refs[n_lefts:]
    sources, refs = refs[:n_sources], refs[n_sources:]
    out, slab, sems, done, done_sems, whole_left, left_sems = refs
    step = pl.program_id(0)
    half = step % 2

    def fetch(at):
        for which, source in enumerate(sources):
            for q in range(2):
                @pl.when(buffer[2 * at + q] == which)
                def _():
                    pltpu.make_async_copy(
                        source.at[position[2 * at + q]], slab.at[at % 2, q], sems.at[at % 2, q]
                    ).start()

    def left_copies(tile):
        depth = ORDER // (n_lefts // 2)
        for at, source in enumerate(lefts):
            rows = pl.ds(at // 2 * depth, depth)
            yield pltpu.make_async_copy(
                source.at[tile], whole_left.at[tile, at % 2, rows, :], left_sems.at[tile, at]
            )

    def written(at, q):
        return pltpu.make_async_copy(
            done.at[at % 2, q], out.at[slots[2 * at + q]], done_sems.at[at % 2, q]
        )

    @pl.when(jnp.logical_and(step == 0, kind[0] == 2))
    def _():
        fetch(0)

    following = jnp.minimum(step + 1, STEPS - 1)

    @pl.when(jnp.logical_and(step + 1 < STEPS, kind[2 * following] == 2))
    def _():
        fetch(following)

    before = jnp.maximum(step - 2, 0)
    for q in range(2):
        @pl.when(jnp.logical_and(step >= 2, kind[2 * before + q] > 0))
        def _():
            written(before, q).wait()

    @pl.when(step == 0)
    def _():
        for copy in left_copies(0):
            copy.start()
        for copy in left_copies(0):
            copy.wait()
        for copy in left_copies(1):
            copy.start()

    @pl.when(step == meta[8])
    def _():
        for copy in left_copies(1):
            copy.wait()

    @pl.when(kind[2 * step] == 2)
    def _():
        tops, rests = [], []
        for q in range(2):
            pltpu.make_async_copy(sources[0].at[0], slab.at[half, q], sems.at[half, q]).wait()
            right = slab[half, q]
            top = right.astype(jnp.bfloat16)
            tops.append(top)
            rests.append((right - top.astype(jnp.float32)).astype(jnp.bfloat16))
        top, rest = jnp.concatenate(tops, 0), jnp.concatenate(rests, 0)
        hi, lo = whole_left[left[step], 0], whole_left[left[step], 1]
        term = product(hi, top) + product(hi, rest) + product(lo, top)
        for j in range(ORDER // ROWS):
            lane = pl.ds(pl.multiple_of(meta[j], ROWS), ROWS)
            rows = slice(j * ROWS, (j + 1) * ROWS)
            for q in range(2):
                done[half, q, lane, :] = trails[q][0, lane, :] - term[rows, q * ROWS : (q + 1) * ROWS]

    @pl.when(kind[2 * step] == 1)
    def _():
        for q in range(2):
            done[half, q] = trails[q][0]

    for q in range(2):
        @pl.when(kind[2 * step + q] > 0)
        def _():
            written(step, q).start()

    @pl.when(step == STEPS - 1)
    def _():
        for at in (STEPS - 2, STEPS - 1):
            for q in range(2):
                @pl.when(kind[2 * at + q] > 0)
                def _():
                    written(at, q).wait()


def product(a, b):
    return lax.dot_general(a, b, (((1,), (1,)), ((), ())), preferred_element_type=jnp.float32)


def update(trailing, lefts, sources, tables):
    def slot(q):
        return lambda step, slots, *_: (slots[2 * step + q], 0, 0)

    hbm = pl.BlockSpec(memory_space=pl.ANY)
    return pl.pallas_call(
        functools.partial(update_kernel, (len(lefts), len(sources))),
        grid_spec=pltpu.PrefetchScalarGridSpec(
            num_scalar_prefetch=len(tables),
            grid=(STEPS,),
            in_specs=[pl.BlockSpec((1, ORDER, ROWS), slot(q)) for q in range(2)]
            + [hbm] * (len(lefts) + len(sources)),
            out_specs=hbm,
            scratch_shapes=[
                pltpu.VMEM((2, 2, ROWS, ORDER), jnp.float32),
                pltpu.SemaphoreType.DMA((2, 2)),
                pltpu.VMEM((2, 2, ORDER, ROWS), jnp.float32),
                pltpu.SemaphoreType.DMA((2, 2)),
                pltpu.VMEM((2, 2, ORDER, ORDER), jnp.bfloat16),
                pltpu.SemaphoreType.DMA((2, len(lefts))),
            ],
        ),
        out_shape=jax.ShapeDtypeStruct(trailing.shape, trailing.dtype),
        compiler_params=pltpu.CompilerParams(vmem_limit_bytes=56 << 20),
    )(*tables, trailing, trailing, *lefts, *sources)


def split(product):
    top = lax.reduce_precision(product, 8, 7)
    flat = (2, product.shape[1] * ROWS, ORDER)
    return top.astype(jnp.bfloat16).reshape(flat), (product - top).astype(jnp.bfloat16).reshape(flat)


def times(blocks, square):
    return split(jnp.einsum("pxak,kj->pxaj", jnp.stack(blocks, 1), square, precision=high))


def per_device(pivot_inverse, panel, trailing, tile_list):
    row, col = lax.axis_index("row"), lax.axis_index("col")
    far, z, core = row // 8, (row // 2) % 4, row % 2
    x, near = col // 2, col % 2
    swap = functools.partial(send, move=to_sibling)

    toward = jnp.where(core == 0, -1, 1)
    places = jnp.stack([x, (x + toward) % 4, (x - toward) % 4, (x + 2) % 4]) * 2
    places = jnp.concatenate([places + near, places + 1 - near]) * ROWS
    left, right = tile_list[:, 0], tile_list[:, 1]
    live = right >= 0
    right = jnp.maximum(right, 0)
    inner, owner = right % 2, right // 2
    owner_far, owner_z, owner_core = owner // 8, (owner // 2) % 4, owner % 2
    dz = (owner_z - z) % 4
    other_core = (owner_core != core).astype(jnp.int32)
    ahead = jnp.where(core == 0, dz == 3, dz == 1)
    here = jnp.where(dz % 2 == 0, dz + other_core, jnp.where(ahead, 4 + other_core, 7 - other_core))
    there = jnp.where(dz % 2 == 0, 8 + dz + other_core, jnp.where(dz == 3, 12, 13) + 2 * other_core)
    buffer = jnp.where(owner_far == far, here, there)
    group = jnp.where(live, left, 2)
    slot = jnp.arange(SLOTS, dtype=jnp.int32)
    ahead_of = (group[None, :] == group[:, None]) & (slot[None, :] < slot[:, None])
    rank = jnp.sum(ahead_of.astype(jnp.int32), 1)
    pairs = [(jnp.sum((group == g).astype(jnp.int32)) + 1) // 2 for g in range(3)]
    start = jnp.where(group == 0, 0, jnp.where(group == 1, pairs[0], pairs[0] + pairs[1]))
    at = 2 * start + rank
    spots = jnp.arange(2 * STEPS, dtype=jnp.int32)
    pick = (at[None, :] == spots[:, None]).astype(jnp.int32)
    mate = (at[None, :] == (spots ^ 1)[:, None]).astype(jnp.int32)
    rows = jnp.stack([slot, buffer, inner, jnp.where(live, 2, 1)]).astype(jnp.int32)
    mine_rows = jnp.sum(rows[:, None, :] * pick[None], 2)
    mate_rows = jnp.sum(rows[:, None, :] * mate[None], 2)
    filled = jnp.sum(pick, 1)
    chosen = jnp.where(filled[None] > 0, mine_rows, mate_rows)
    kind = jnp.where(filled > 0, chosen[3], 0)
    left_of = jnp.where(jnp.arange(STEPS, dtype=jnp.int32) < pairs[0], 0, 1).astype(jnp.int32)
    meta = jnp.concatenate([places, pairs[0][None]]).astype(jnp.int32)
    tables = [chosen[0], left_of, chosen[1], chosen[2], kind, meta]

    half = ORDER // 2

    sib = swap(panel)
    other = send(pivot_inverse, far_y)
    near_own = send(after(panel, other), near_y)
    z1a = send(panel, along_z)
    upper = jnp.where(far == 0, pivot_inverse, other)[:, :half]
    lower = jnp.where(far == 0, other, pivot_inverse)
    mine = jnp.concatenate([lower, upper], 1)
    x1a = send(panel, along_x)
    x1b = send(sib, along_x)
    z1b = send(sib, along_z)
    mine = after(mine, x1a, z1a)
    from_down = send(mine, turn_z(1))
    from_up = send(mine, turn_z(-1))

    done = (x1a, x1b, z1a, z1b, near_own, from_down, from_up, *tables)
    z2 = send(after(z1a, *done), along_z)
    across = send(after(mine, *done), turn_z(2))
    x2n = send(after(jnp.concatenate([x1a, near_own], 0), *done), along_x)
    far_own = send(after(panel, *done), far_y)
    quarters = jnp.stack([mine, from_up, across, from_down], 0)
    both_sib = swap(after(jnp.concatenate([near_own, x1b], 0), *done))
    near_sib, sx1 = both_sib[:2], both_sib[2:]
    x2, nx1a = x2n[:2], x2n[2:]

    done = (z2, across, x2n, far_own, both_sib)
    near_pair = after(jnp.concatenate([near_sib, nx1a], 0), *done)
    nx12 = send(near_pair, along_x)
    theirs = swap(after(quarters, near_pair))
    sz1a, sz1b = swap(after(z1a, theirs)), swap(after(z1b, theirs))
    fz_down = send(after(far_own, near_pair), turn_z(1))
    fz_up = send(after(far_own, near_pair), turn_z(-1))
    fz2 = send(after(z2, near_pair), far_y)
    sz2, far_sib = swap(after(z2, theirs)), swap(after(far_own, theirs))
    nx1b, nx2 = nx12[:2], nx12[2:]

    first = jnp.where(core == 0, quarters, theirs)
    second = jnp.where(core == 0, theirs, quarters)
    whole = jnp.stack([first, second], 1).reshape(half, ORDER + half)
    lower, upper = whole[:, :ORDER], whole[:, ORDER:]
    square = square_of(lower, upper)
    own_first = times([panel, x1a], square)
    own_second = times([sx1, x2], square)
    near_first = times([near_own, nx1a], square)
    solved = solve(panel, lower, upper, z)
    ready = (solved[0, :8, :ROWS], *own_first, *near_first)
    nsx1 = swap(after(nx1b, *ready))
    near_second = times([nsx1, nx2], square)
    sfz_down, sfz_up, sfz2 = [swap(after(part, *ready, *own_second)) for part in (fz_down, fz_up, fz2)]

    sources = [panel, sib, z2, sz2, z1a, z1b, sz1a, sz1b]
    sources += [far_own, far_sib, fz2, sfz2, fz_down, fz_up, sfz_down, sfz_up]
    lefts = own_first + own_second + near_first + near_second
    return solved, update(trailing, lefts, sources, tables)


def solution(mesh):
    placed = (P("row", None), P("row", "col", None), P("row", None, "col"), P("row", None))
    return jax.shard_map(
        per_device,
        mesh=mesh,
        in_specs=placed,
        out_specs=(P("row", "col", None), P("row", None, "col")),
        check_vma=False,
    )
```
